128 devices in a mesh: req: 8 (over x, core), tok: 16 (over y, z).
Axes of the slice: x: 4, y: 4, z: 4, core: 2. Of those that a mesh axis runs over, the one named last changes fastest.
Arguments:
- hidden_in: bfloat16 [8, 2048, 2048], P('req', 'tok'), may hold values from -6 to 6
- attention_gain: bfloat16 [2048], replicated, may hold values from 0.25 to 1.75
- attend_matrix: bfloat16 [2048, 2560], P(None, 'req'), may hold values from -0.125 to 0.125
- merge_matrix: bfloat16 [2048, 2048], P('req'), may hold values from -1 to 1
- feedforward_gain: bfloat16 [2048], replicated, may hold values from 0.25 to 1.75
- gate_matrix: bfloat16 [2048, 8192], P(None, 'tok'), may hold values from -0.125 to 0.125
- up_matrix: bfloat16 [2048, 8192], P(None, 'tok'), may hold values from -0.125 to 0.125
- down_matrix: bfloat16 [8192, 2048], P('tok'), may hold values from -0.0625 to 0.0625
- kv_pool: bfloat16 [8, 48, 2, 128, 256], P('req', 'tok'), may hold values from -320 to 320
- lengths: int32 [8], P('req'), may hold values from 0 to 16384, as said below
- page_table: int32 [8, 16], P('req'), may hold values from 0 to 47, as said below
- free_slots: int32 [8, 16], P('req'), may hold values from 0 to 47, as said below
Outputs:
- layer_output: bfloat16 [8, 2048, 2048], P('req', 'tok')
- updated_pool: bfloat16 [8, 48, 2, 128, 256], P('req', 'tok')
The draws below stay inside these ranges and needn't reach their ends.
Inputs may be any that keep to these rules, and one draw needn't show every extreme that they name: `lengths`: multiples of 128; in every draw some request has 0 and some has 16384. For each request the entries of its page_table row and of its free_slots row are all distinct slots of its pool. `free_slots`: see page_table.
All inputs are finite; a program needn't handle non-finite values.
Results may differ from the reference program's by a relative error of at most 0.018.
The reference program's roundings to bfloat16 on the way count: a program that leaves them out, or rounds other values in their place, can miss the bound.
Values may be sent and summed in bfloat16 or wider, within the bound.
A program may use at most 192 MiB of HBM per device.

```python
import math
import jax
import jax.numpy as jnp
from jax import lax

D = 2048
HEADS = 32
KV_HEADS = 4
HEAD_DIM = 64
FF = 8192
WINDOW = 2048
PAGE = 128
MAXLEN = 16384
SPAN = 2048
POOL = 48
REQUESTS = 8
QW = 2048
KVW = 256
WPAGES = 16
NPAGES = 16
N_TOK = 16


def slot_orders(key):
    row_keys = jax.random.split(jax.random.fold_in(key, 11), REQUESTS)

    def one_order(row_key):
        return jax.random.permutation(row_key, POOL)
    orders = jax.vmap(one_order)(row_keys).astype(jnp.int32)
    picks = jax.random.permutation(jax.random.fold_in(key, 13), REQUESTS)
    row_ids = jnp.arange(REQUESTS)
    shift_table = jnp.where(row_ids == picks[0], orders[:, 0], jnp.where(row_ids == picks[1], orders[:, 0] + 1, 0))
    shift_free = jnp.where(row_ids == picks[2], orders[:, WPAGES], jnp.where(row_ids == picks[3], orders[:, WPAGES] + 1, 0))
    return ((orders - (shift_table + shift_free)[:, None]) % POOL).astype(jnp.int32)


def draw_page_table(key, part):
    return slot_orders(key)[:, :WPAGES]


def draw_free_slots(key, part):
    return slot_orders(key)[:, WPAGES:WPAGES + NPAGES]


def draw_lengths(key, part):
    raw = PAGE * jax.random.randint(jax.random.fold_in(key, 17), (REQUESTS,), 0, MAXLEN // PAGE + 1)
    picks = jax.random.permutation(jax.random.fold_in(key, 19), REQUESTS)
    row_ids = jnp.arange(REQUESTS)
    raw = jnp.where(row_ids == picks[0], MAXLEN, jnp.where(row_ids == picks[1], 0, raw))
    return raw.astype(jnp.int32)


def draw_kv_pool(key, part):
    base = jax.random.truncated_normal(jax.random.fold_in(key, 23), -4.0, 4.0, (REQUESTS, POOL, 2, PAGE, KVW), jnp.float32)
    return base.astype(jnp.bfloat16)


def block_scale(stream_key, dims, shards, smallest, largest):
    def one(position, blocks):
        heights = jax.random.uniform(jax.random.fold_in(jax.random.fold_in(stream_key, 6), position), (blocks,), jnp.float32, smallest / len(shards), largest / len(shards))
        return jnp.repeat(jnp.exp(heights), dims[position] // blocks).reshape((-1,) + (1,) * (len(dims) - position - 1))

    loudness = one(*shards[0])
    for cut in shards[1:]:
        loudness = loudness * one(*cut)
    return loudness


def bell_draw(rng, extent, width, limit, cuts=(), held_as=jnp.bfloat16):
    entries = jax.random.normal(rng, extent, jnp.float32) * width
    if len(cuts) > 0:
        entries = block_scale(rng, extent, cuts, -0.22, 0.18) * entries
    return jnp.clip(entries, min=-limit, max=limit).astype(held_as)


def setup_inputs(seed: int = 0) -> dict:
    key_of = jax.random.split(jax.random.key(seed), 13)
    return {
        "hidden_in": bell_draw(key_of[0], (REQUESTS, SPAN, D), 1.0, 6.0, ((0, 8), (1, 16))),
        "attention_gain": jnp.clip(1.0 + 0.15 * jax.random.normal(key_of[1], (D,), jnp.float32), 0.25, 1.75).astype(jnp.bfloat16),
        "attend_matrix": bell_draw(key_of[2], (D, QW + 2 * KVW), D ** -0.5, 0.125, ((1, 8),)),
        "merge_matrix": bell_draw(key_of[3], (QW, D), (max(1, QW // 64)) ** -0.5, 1.0, ((0, 8),)),
        "feedforward_gain": jnp.clip(1.0 + 0.15 * jax.random.normal(key_of[4], (D,), jnp.float32), 0.25, 1.75).astype(jnp.bfloat16),
        "gate_matrix": bell_draw(key_of[5], (D, FF), D ** -0.5, 0.125, ((1, 16),)),
        "up_matrix": bell_draw(key_of[6], (D, FF), D ** -0.5, 0.125, ((1, 16),)),
        "down_matrix": bell_draw(key_of[7], (FF, D), FF ** -0.5, 0.0625, ((0, 16),)),
        "kv_pool": draw_kv_pool(jax.random.fold_in(key_of[12], 71), 0),
        "lengths": draw_lengths(jax.random.fold_in(key_of[12], 71), 0),
        "page_table": draw_page_table(jax.random.fold_in(key_of[12], 71), 0),
        "free_slots": draw_free_slots(jax.random.fold_in(key_of[12], 71), 0),
    }


epsilon = 1e-05
rope_base = 10000.0

def rms_scale(matrix, gain):
    values = matrix.astype(jnp.float32)
    inverse = lax.rsqrt(lax.optimization_barrier(jnp.mean(values * values, axis=-1, keepdims=True)) + epsilon)
    return (values * inverse * gain.astype(jnp.float32)).astype(jnp.bfloat16)

def rotate(values, positions):
    half_dim = values.shape[-1] // 2
    frequency = rope_base ** (-2.0 * jnp.arange(half_dim, dtype=jnp.float32) / values.shape[-1])
    angles = positions.astype(jnp.float32)[:, None] * frequency[None, :]
    cosine = jnp.cos(angles)[:, None, :]
    sine_part = jnp.sin(angles)[:, None, :]
    lower_half = values[..., :half_dim]
    upper_half = values[..., half_dim:]
    return jnp.concatenate([lower_half * cosine - upper_half * sine_part, upper_half * cosine + lower_half * sine_part], axis=-1)

def attend(queries, all_keys, all_values, query_pos, key_pos):
    row_count = queries.shape[0]
    group_size = HEADS // KV_HEADS
    allowed = (key_pos[None, :] >= 0) & (key_pos[None, :] <= query_pos[:, None]) & (key_pos[None, :] > query_pos[:, None] - WINDOW)
    factor = 1.0 / math.sqrt(HEAD_DIM)
    blocks = []
    for head_index in range(KV_HEADS):
        query_block = queries[:, head_index * group_size * HEAD_DIM:(head_index + 1) * group_size * HEAD_DIM].reshape(row_count * group_size, HEAD_DIM)
        key_block = all_keys[:, head_index * HEAD_DIM:(head_index + 1) * HEAD_DIM]
        value_block = all_values[:, head_index * HEAD_DIM:(head_index + 1) * HEAD_DIM]
        scores = lax.dot_general(query_block, key_block, (((1,), (1,)), ((), ())), preferred_element_type=jnp.float32) * factor
        scores = jnp.where(allowed[:, None, :], scores.reshape(row_count, group_size, -1), -jnp.inf)
        row_peak = lax.optimization_barrier(jnp.max(scores, axis=-1, keepdims=True))
        weights = jnp.exp(scores - row_peak)
        row_total = lax.optimization_barrier(jnp.sum(weights, axis=-1, keepdims=True))
        weighted = jnp.dot(weights.astype(jnp.bfloat16).reshape(row_count * group_size, -1), value_block, preferred_element_type=jnp.float32)
        blocks.append(weighted.reshape(row_count, group_size, HEAD_DIM) / row_total)
    return jnp.concatenate(blocks, axis=1).reshape(row_count, HEADS * HEAD_DIM).astype(jnp.bfloat16)

def reference(hidden_in, attention_gain, attend_matrix, merge_matrix, feedforward_gain, gate_matrix, up_matrix, down_matrix, kv_pool, lengths, page_table, free_slots):
    query_width = HEADS * HEAD_DIM
    kv_width = KV_HEADS * HEAD_DIM
    shard_width = FF // N_TOK

    def one_request(packed):
        tokens, length, table, free_ids, pool = packed
        normed = rms_scale(tokens, attention_gain)
        projected = jnp.dot(normed, attend_matrix, preferred_element_type=jnp.float32)
        positions = length + jnp.arange(SPAN, dtype=jnp.int32)
        queries = rotate(projected[:, :query_width].reshape(SPAN, HEADS, HEAD_DIM), positions).astype(jnp.bfloat16).reshape(SPAN, query_width)
        new_keys = rotate(projected[:, query_width:query_width + kv_width].reshape(SPAN, KV_HEADS, HEAD_DIM), positions).astype(jnp.bfloat16).reshape(SPAN, kv_width)
        new_values = projected[:, query_width + kv_width:].astype(jnp.bfloat16)
        fresh = jnp.stack([new_keys, new_values])
        window = jnp.transpose(pool[table], (1, 0, 2, 3)).reshape(2, WINDOW, kv_width)
        all_keys = jnp.concatenate([window[0], fresh[0]], axis=0)
        all_values = jnp.concatenate([window[1], fresh[1]], axis=0)
        key_pos = jnp.concatenate([length - WINDOW + jnp.arange(WINDOW, dtype=jnp.int32), positions])
        attended = attend(queries, all_keys, all_values, positions, key_pos)
        merged = jnp.dot(attended, merge_matrix, preferred_element_type=jnp.float32)
        residual = (tokens.astype(jnp.float32) + merged).astype(jnp.bfloat16)
        normed_two = rms_scale(residual, feedforward_gain)
        gate = jnp.dot(normed_two, gate_matrix, preferred_element_type=jnp.float32)
        lifted = jnp.dot(normed_two, up_matrix, preferred_element_type=jnp.float32)
        inner = (jax.nn.silu(gate) * lifted).astype(jnp.bfloat16)
        inner_blocks = jnp.transpose(inner.reshape(SPAN, N_TOK, shard_width), (1, 0, 2))
        down_blocks = down_matrix.reshape(N_TOK, shard_width, D)

        def add_block(running, operands):
            partial_value = jnp.dot(operands[0], operands[1], preferred_element_type=jnp.float32).astype(jnp.bfloat16)
            partial_value = lax.optimization_barrier(partial_value)
            return (running + partial_value.astype(jnp.float32), None)
        feed_sum = lax.scan(add_block, jnp.zeros((SPAN, D), jnp.float32), (inner_blocks, down_blocks))[0]
        output_rows = (residual.astype(jnp.float32) + feed_sum).astype(jnp.bfloat16)
        new_pages = jnp.transpose(fresh.reshape(2, SPAN // PAGE, PAGE, kv_width), (1, 0, 2, 3))
        new_pool = pool.at[free_ids].set(new_pages)
        return (output_rows, new_pool)
    results = lax.map(one_request, (hidden_in, lengths, page_table, free_slots, kv_pool))
    return (results[0], results[1])
```

```python
import math

import jax
import jax.numpy as jnp
from jax import lax
from jax.experimental import pallas as pl
from jax.experimental.pallas import tpu as pltpu
from jax.sharding import PartitionSpec as P

HEADS = 32
KV_HEADS = 4
HEAD_DIM = 64
WINDOW = 2048
PAGE = 128
SPAN = 2048
D = 2048
FF_LOCAL = 512
QW = HEADS * HEAD_DIM
KVW = KV_HEADS * HEAD_DIM
WPAGES = WINDOW // PAGE
SEEN = WPAGES + 1
N_TOK = 16

epsilon = 1e-05
rope_base = 10000.0
MASKED = -1e30


def rms_scale(matrix, gain):
    values = matrix.astype(jnp.float32)
    inverse = lax.rsqrt(jnp.mean(values * values, axis=-1, keepdims=True) + epsilon)
    return (values * inverse * gain.astype(jnp.float32)).astype(jnp.bfloat16)


def rope_tables(positions):
    half_dim = HEAD_DIM // 2
    frequency = rope_base ** (-2.0 * jnp.arange(half_dim, dtype=jnp.float32) / HEAD_DIM)
    angles = positions.astype(jnp.float32)[:, None] * frequency[None, :]
    cosine = jnp.cos(angles)
    sine = jnp.sin(angles)
    return (
        jnp.concatenate([cosine] * 4, axis=1),
        jnp.concatenate([-sine, sine, -sine, sine], axis=1),
    )


def rope_slab(slab, cosine, sine):
    lane = lax.broadcasted_iota(jnp.int32, slab.shape, 1)
    swapped = jnp.where(lane % 64 < 32, pltpu.roll(slab, 96, 1), pltpu.roll(slab, 32, 1))
    return slab * cosine + swapped * sine


def attention_kernel(
    table_ref,
    free_ref,
    length_ref,
    proj_ref,
    cos_ref,
    sin_ref,
    pool_ref,
    span_ref,
    local_ref,
    out_ref,
    new_ref,
    kbuf,
    vbuf,
    bias,
    page_sems,
    slot_sems,
):
    t = lax.axis_index("tok")
    slots = new_ref.shape[0]

    def page_copy(g, kv, source):
        target = (kbuf if kv == 0 else vbuf).at[pl.ds(pl.multiple_of(g * PAGE, PAGE), PAGE)]
        return pltpu.make_async_copy(source, target, page_sems.at[g, kv])

    def fetch(g, carry):
        page = t + g

        @pl.when(page < WPAGES)
        def _():
            slot = table_ref[jnp.minimum(page, WPAGES - 1)]
            for kv in range(2):
                page_copy(g, kv, pool_ref.at[slot, kv]).start()

        @pl.when(page >= WPAGES)
        def _():
            rows = pl.ds(pl.multiple_of(jnp.maximum(page - WPAGES, 0) * PAGE, PAGE), PAGE)
            for kv in range(2):
                page_copy(g, kv, span_ref.at[kv, rows]).start()

        return carry

    lax.fori_loop(0, SEEN, fetch, 0)

    for s in range(slots):
        slot_id = t * slots + s
        found = jnp.int32(-1)
        for j in range(N_TOK):
            found = jnp.where(free_ref[j] == slot_id, j, found)

        @pl.when(found >= 0)
        def _():
            rows = pl.ds(pl.multiple_of(jnp.maximum(found, 0) * PAGE, PAGE), PAGE)
            for kv in range(2):
                pltpu.make_async_copy(
                    span_ref.at[kv, rows], new_ref.at[s, kv], slot_sems.at[s, kv]
                ).start()

        @pl.when(found < 0)
        def _():
            for kv in range(2):
                pltpu.make_async_copy(
                    local_ref.at[s, kv], new_ref.at[s, kv], slot_sems.at[s, kv]
                ).start()

    row = lax.broadcasted_iota(jnp.int32, (PAGE, SEEN * PAGE), 0)
    column = lax.broadcasted_iota(jnp.int32, (PAGE, SEEN * PAGE), 1)
    first = jnp.maximum((WINDOW - length_ref[0]) - t * PAGE, 0)
    allowed = (column > row) & (column <= row + WINDOW) & (column >= first)
    bias[...] = jnp.where(allowed, 0.0, MASKED)

    def drain(g, carry):
        for kv in range(2):
            page_copy(g, kv, pool_ref.at[0, kv]).wait()
        return carry

    lax.fori_loop(0, SEEN, drain, 0)

    lane = lax.broadcasted_iota(jnp.int32, (PAGE, 128), 1)
    low = lane < 64
    factor = math.log2(math.e) / math.sqrt(HEAD_DIM)

    def pair_step(pair, carry):
        columns = pl.ds(pl.multiple_of(pair * 128, 128), 128)
        shared = pl.ds(pl.multiple_of((pair // 8) * 128, 128), 128)
        even_group = (pair // 4) % 2 == 0
        slab = rope_slab(proj_ref[:, columns], cos_ref[...], sin_ref[...])
        turned = pltpu.roll(slab, 64, 1)
        query_one = jnp.where(even_group, jnp.where(low, slab, 0.0), jnp.where(low, 0.0, turned))
        query_two = jnp.where(even_group, jnp.where(low, turned, 0.0), jnp.where(low, 0.0, slab))
        both = jnp.concatenate([query_one, query_two], axis=0).astype(jnp.bfloat16)
        scores = lax.dot_general(
            both, kbuf[:, shared], (((1,), (1,)), ((), ())), preferred_element_type=jnp.float32
        )
        scores = scores.reshape(2, PAGE, SEEN * PAGE) * factor + bias[...][None]
        peak = jnp.max(scores, axis=-1, keepdims=True)
        weights = jnp.exp2(scores - peak)
        total = jnp.sum(weights, axis=-1, keepdims=True)
        weighted = jnp.dot(
            weights.astype(jnp.bfloat16).reshape(2 * PAGE, SEEN * PAGE),
            vbuf[:, shared],
            preferred_element_type=jnp.float32,
        ).reshape(2, PAGE, 128)
        weighted = weighted / total
        one, two = weighted[0], weighted[1]
        left = jnp.where(even_group, one, pltpu.roll(one, 64, 1))
        right = jnp.where(even_group, pltpu.roll(two, 64, 1), two)
        out_ref[:, columns] = jnp.where(low, left, right).astype(jnp.bfloat16)
        return carry

    lax.fori_loop(0, HEADS // 2, pair_step, 0)

    for s in range(slots):
        for kv in range(2):
            pltpu.make_async_copy(
                local_ref.at[s, kv], new_ref.at[s, kv], slot_sems.at[s, kv]
            ).wait()


def attention(table, free, length, projected, cosine, sine, pool, span, pool_local):
    vmem = pl.BlockSpec(memory_space=pltpu.VMEM)
    smem = pl.BlockSpec(memory_space=pltpu.SMEM)
    hbm = pl.BlockSpec(memory_space=pl.ANY)
    rows = projected.shape[0]
    return pl.pallas_call(
        attention_kernel,
        name="window_attention",
        out_shape=(
            jax.ShapeDtypeStruct((rows, QW), jnp.bfloat16),
            jax.ShapeDtypeStruct(pool_local.shape, jnp.bfloat16),
        ),
        in_specs=[smem, smem, smem, vmem, vmem, vmem, hbm, hbm, hbm],
        out_specs=(vmem, vmem),
        scratch_shapes=[
            pltpu.VMEM((SEEN * PAGE, KVW), jnp.bfloat16),
            pltpu.VMEM((SEEN * PAGE, KVW), jnp.bfloat16),
            pltpu.VMEM((PAGE, SEEN * PAGE), jnp.float32),
            pltpu.SemaphoreType.DMA((SEEN, 2)),
            pltpu.SemaphoreType.DMA((pool_local.shape[0], 2)),
        ],
        compiler_params=pltpu.CompilerParams(vmem_limit_bytes=40 << 20),
        cost_estimate=pl.CostEstimate(
            flops=4 * rows * HEADS * SEEN * PAGE * 128,
            bytes_accessed=8 << 20,
            transcendentals=rows * HEADS * SEEN * PAGE,
        ),
    )(table, free, length, projected, cosine, sine, pool, span, pool_local)


RINGS = 4
PART = PAGE // RINGS
HALF = D // 2


def ring_neighbours():
    t = lax.axis_index("tok")
    y, z = t // 4, t % 4

    def at(row, column):
        return ((row + 4) % 4) * 4 + (column + 4) % 4

    down_one = jnp.where((z + y) % 4 == 3, at(y + 1, z), at(y, z + 1))
    up_one = jnp.where((z + y) % 4 == 0, at(y - 1, z), at(y, z - 1))
    down_two = jnp.where((z + y) % 4 == 3, at(y, z + 1), at(y + 1, z))
    up_two = jnp.where((z + y) % 4 == 0, at(y, z - 1), at(y - 1, z))
    return (down_one, up_one, down_two, up_two)


def feed_kernel(
    resid_ref,
    gain_ref,
    gate_ref,
    up_ref,
    down_ref,
    out_ref,
    tok,
    inc,
    pout,
    acc,
    tok_send,
    tok_recv,
    sum_send,
    sum_recv,
):
    targets = ring_neighbours()

    def part(r):
        return pl.ds(r * PART, PART)

    def token_copy(k, r):
        return pltpu.make_async_remote_copy(
            src_ref=tok.at[k, part(r)],
            dst_ref=tok.at[k + 1, part(r)],
            send_sem=tok_send.at[k, r],
            recv_sem=tok_recv.at[k, r],
            device_id={"tok": targets[r]},
            device_id_type=pl.DeviceIdType.MESH,
        )

    def sum_copy(k, half, r):
        return pltpu.make_async_remote_copy(
            src_ref=pout.at[k % 2, half, part(r)],
            dst_ref=inc.at[k - 1, half, part(r)],
            send_sem=sum_send.at[k - 1, half, r],
            recv_sem=sum_recv.at[k - 1, half, r],
            device_id={"tok": targets[r]},
            device_id_type=pl.DeviceIdType.MESH,
        )

    barrier = pltpu.get_barrier_semaphore()
    for target in targets:
        pl.semaphore_signal(
            barrier, inc=1, device_id={"tok": target}, device_id_type=pl.DeviceIdType.MESH
        )

    values = resid_ref[...].astype(jnp.float32)
    inverse = lax.rsqrt(jnp.mean(values * values, axis=-1, keepdims=True) + epsilon)
    tok[0] = (values * inverse * gain_ref[...].astype(jnp.float32)).astype(jnp.bfloat16)

    pl.semaphore_wait(barrier, RINGS)
    for r in range(RINGS):
        token_copy(0, r).start()

    def inner_of(k):
        rows = tok[k]
        gate = jnp.dot(rows, gate_ref[...], preferred_element_type=jnp.float32)
        lifted = jnp.dot(rows, up_ref[...], preferred_element_type=jnp.float32)
        return (gate / (1.0 + jnp.exp(-gate)) * lifted).astype(jnp.bfloat16)

    inner = inner_of(0)
    for half in range(2):
        acc[half] = jnp.dot(
            inner, down_ref[:, half * HALF : (half + 1) * HALF], preferred_element_type=jnp.float32
        )

    def step(k, carry):
        for r in range(RINGS):
            token_copy(k - 1, r).wait_recv()

        @pl.when(k < N_TOK - 1)
        def _():
            for r in range(RINGS):
                token_copy(k, r).start()

        inner = inner_of(k)
        for half in range(2):
            term = jnp.dot(
                inner,
                down_ref[:, half * HALF : (half + 1) * HALF],
                preferred_element_type=jnp.float32,
            )

            @pl.when(k > 2)
            def _():
                for r in range(RINGS):
                    sum_copy(k - 2, half, r).wait_send()

            @pl.when(k > 1)
            def _():
                for r in range(RINGS):
                    sum_copy(k - 1, half, r).wait_recv()
                pout[k % 2, half] = (inc[k - 2, half].astype(jnp.float32) + term).astype(
                    jnp.bfloat16
                )

            @pl.when(k == 1)
            def _():
                pout[k % 2, half] = term.astype(jnp.bfloat16)

            for r in range(RINGS):
                sum_copy(k, half, r).start()
        return carry

    lax.fori_loop(1, N_TOK, step, 0)

    last = N_TOK - 1
    for half in range(2):
        columns = slice(half * HALF, (half + 1) * HALF)
        for r in range(RINGS):
            sum_copy(last, half, r).wait_recv()
        feed = inc[last - 1, half].astype(jnp.float32) + acc[half]
        out_ref[:, columns] = (resid_ref[:, columns].astype(jnp.float32) + feed).astype(
            jnp.bfloat16
        )
    for half in range(2):
        for r in range(RINGS):
            sum_copy(last - 1, half, r).wait_send()
            sum_copy(last, half, r).wait_send()

    def drain(k, carry):
        for r in range(RINGS):
            token_copy(k, r).wait_send()
        return carry

    lax.fori_loop(0, N_TOK - 1, drain, 0)


def feed_forward(residual, gain, gate, up, down):
    vmem = pl.BlockSpec(memory_space=pltpu.VMEM)
    rows = residual.shape[0]
    return pl.pallas_call(
        feed_kernel,
        name="ring_feed_forward",
        out_shape=jax.ShapeDtypeStruct((rows, D), jnp.bfloat16),
        in_specs=[vmem] * 5,
        out_specs=vmem,
        scratch_shapes=[
            pltpu.VMEM((N_TOK, PAGE, D), jnp.bfloat16),
            pltpu.VMEM((N_TOK - 1, 2, PAGE, HALF), jnp.bfloat16),
            pltpu.VMEM((2, 2, PAGE, HALF), jnp.bfloat16),
            pltpu.VMEM((2, PAGE, HALF), jnp.float32),
            pltpu.SemaphoreType.DMA((N_TOK - 1, RINGS)),
            pltpu.SemaphoreType.DMA((N_TOK - 1, RINGS)),
            pltpu.SemaphoreType.DMA((N_TOK - 1, 2, RINGS)),
            pltpu.SemaphoreType.DMA((N_TOK - 1, 2, RINGS)),
        ],
        compiler_params=pltpu.CompilerParams(
            collective_id=0, has_side_effects=True, vmem_limit_bytes=48 << 20
        ),
    )(residual, gain.reshape(1, D), gate, up, down)


def rotate_keys(keys, cosine, sine):
    rows = keys.shape[0]
    parts = keys.reshape(rows, KV_HEADS, 2, HEAD_DIM // 2)
    cos = cosine[:, None, : HEAD_DIM // 2]
    sin = sine[:, None, HEAD_DIM // 2 : HEAD_DIM]
    lower, upper = parts[:, :, 0], parts[:, :, 1]
    return jnp.concatenate(
        [lower * cos - upper * sin, upper * cos + lower * sin], axis=-1
    ).reshape(rows, KVW)


def shards(
    hidden_in,
    attention_gain,
    attend_matrix,
    merge_matrix,
    feedforward_gain,
    gate_matrix,
    up_matrix,
    down_matrix,
    kv_pool,
    lengths,
    page_table,
    free_slots,
):
    tokens = hidden_in[0]
    tok_rows = tokens.shape[0]
    tok_index = lax.axis_index("tok")
    normed = rms_scale(tokens, attention_gain)
    projected = jnp.dot(
        normed,
        lax.all_gather(attend_matrix, "req", axis=1, tiled=True),
        preferred_element_type=jnp.float32,
    )
    positions = lengths[0] + tok_index * tok_rows + jnp.arange(tok_rows, dtype=jnp.int32)
    cosine, sine = rope_tables(positions)
    new_keys = rotate_keys(projected[:, QW : QW + KVW], cosine, sine).astype(jnp.bfloat16)
    new_values = projected[:, QW + KVW :].astype(jnp.bfloat16)
    fresh = jnp.stack([new_keys, new_values])
    pool_local = kv_pool[0]
    whole_pool = lax.all_gather(pool_local, "tok", axis=0, tiled=True)
    span_kv = lax.all_gather(fresh, "tok", axis=1, tiled=True)
    attended, new_local = attention(
        page_table[0],
        free_slots[0],
        lengths,
        projected,
        cosine,
        sine,
        whole_pool,
        span_kv,
        pool_local,
    )
    merged = jnp.dot(
        attended,
        lax.all_gather(merge_matrix, "req", axis=0, tiled=True),
        preferred_element_type=jnp.float32,
    )
    residual = (tokens.astype(jnp.float32) + merged).astype(jnp.bfloat16)
    output_rows = feed_forward(residual, feedforward_gain, gate_matrix, up_matrix, down_matrix)
    return (output_rows[None], new_local[None])


def solution(mesh):
    in_specs = (
        P("req", "tok", None),
        P(),
        P(None, "req"),
        P("req", None),
        P(),
        P(None, "tok"),
        P(None, "tok"),
        P("tok", None),
        P("req", "tok", None, None, None),
        P("req"),
        P("req", None),
        P("req", None),
    )
    out_specs = (P("req", "tok", None), P("req", "tok", None, None, None))
    return jax.shard_map(shards, mesh=mesh, in_specs=in_specs, out_specs=out_specs, check_vma=False)
```
